256 devices in a mesh: sec: 8 (over z), chan: 32 (over y, x, core).
Axes of the slice: x: 4, y: 4, z: 8, core: 2. Of those that a mesh axis runs over, the one named last changes fastest.
Arguments:
- state_blocks: bfloat16 [8, 512, 512], P('sec'), may hold values from -6 to 6
- left_blocks: bfloat16 [256, 8, 512, 512], P('chan', 'sec'), may hold values from -0.25 to 0.25
- right_blocks: bfloat16 [256, 8, 512, 512], P('chan', 'sec'), may hold values from -0.25 to 0.25
- widths: int32 [8], P('sec'), may hold values from 128 to 512
- step_sizes: float32 [8], P('sec'), may hold values from 0.1 to 0.4
- shifts: int32 [256], P('chan'), may hold values from -1 to 1
Outputs:
- update: bfloat16 [8, 512, 512], P('sec', 'chan')
- new_left: bfloat16 [256, 8, 512, 512], P('chan', 'sec')
The draws below stay inside these ranges and needn't reach their ends.
All inputs are finite; a program needn't handle non-finite values.
Results may differ from the reference program's by a relative error of at most 0.012.
Values may be sent and summed in bfloat16 or wider, within the bound.
A program may use at most 64 MiB of HBM per device.

```python
import math
import jax
import jax.numpy as jnp
from jax import lax

PAD = 512
REACH = 1
SECTORS = 8
CHANNELS = 256


def plant(drawn, key, least, high):
    place = [jax.random.randint(jax.random.fold_in(key, axis), (), 0, length) for axis, length in enumerate(drawn.shape)]
    main_axis = drawn.shape.index(max(drawn.shape))
    beside = place[:main_axis] + [(place[main_axis] + 1) % drawn.shape[main_axis]] + place[main_axis + 1:]
    return drawn.at[tuple(place)].set(least).at[tuple(beside)].set(high)


def block_scale(key, shape, shards, low, high):
    factor_of = 1.0
    for axis_at, blocks in shards:
        draws = jax.random.uniform(jax.random.fold_in(jax.random.fold_in(key, 6), axis_at), (blocks,), jnp.float32, low / len(shards), high / len(shards))
        factor_of = factor_of * jnp.repeat(jnp.exp(draws), shape[axis_at] // blocks).reshape((-1,) + (1,) * (len(shape) - 1 - axis_at))
    return factor_of


def scatter_about(rng, shape, width, limit, split=(), kind=jnp.bfloat16):
    values = jax.random.normal(rng, shape, jnp.float32) * width
    if len(split) > 0:
        values = block_scale(rng, shape, split, -0.22, 0.18) * values
    return jnp.clip(values, min=-limit, max=limit).astype(kind)


def setup_inputs(seed: int = 0) -> dict:
    arg_keys = jax.random.split(jax.random.key(seed), 7)
    return {
        "state_blocks": scatter_about(arg_keys[0], (SECTORS, PAD, PAD), 1.0, 6.0, ((0, 8),)),
        "left_blocks": scatter_about(arg_keys[1], (CHANNELS, SECTORS, PAD, PAD), PAD ** -0.5, 0.25, ((0, 32), (1, 8))),
        "right_blocks": scatter_about(arg_keys[2], (CHANNELS, SECTORS, PAD, PAD), PAD ** -0.5, 0.25, ((0, 32), (1, 8))),
        "widths": plant(jax.random.randint(arg_keys[3], (SECTORS,), PAD // 4, PAD + 1), jax.random.fold_in(arg_keys[3], 1), PAD // 4, PAD).astype(jnp.int32),
        "step_sizes": jnp.clip(jnp.exp(math.log(0.4) - 1.3862944 * jax.random.uniform(arg_keys[4], (SECTORS,), jnp.float32) ** block_scale(arg_keys[4], (SECTORS,), ((0, 8),), -0.2, 0.2)), 0.1, 0.4),
        "shifts": plant(jax.random.randint(arg_keys[5], (CHANNELS,), -REACH, REACH + 1), jax.random.fold_in(arg_keys[5], 1), -REACH, REACH).astype(jnp.int32),
    }


def reference(state_blocks, left_blocks, right_blocks, widths, step_sizes, shifts):
    positions = jnp.arange(PAD, dtype=jnp.int32)
    within = positions[None, :] < widths[:, None]
    inside = within[:, :, None] & within[:, None, :]
    states = jnp.where(inside, state_blocks, jnp.zeros_like(state_blocks))
    sectors = jnp.arange(SECTORS, dtype=jnp.int32)

    def pick(blocks, offset):
        source = sectors - offset
        valid = (source >= 0) & (source < SECTORS)
        taken = blocks[jnp.clip(source, 0, SECTORS - 1).astype(jnp.int32)]
        return jnp.where(valid[:, None, None], taken, jnp.zeros_like(taken))

    def matvec_step(total, pieces):
        left, right, offset = pieces
        source = pick(states, offset)
        halfway = jnp.einsum("sab,sbd->sad", left.astype(jnp.float32), source.astype(jnp.float32)).astype(jnp.bfloat16)
        second = jnp.einsum("sad,sed->sae", halfway.astype(jnp.float32), right.astype(jnp.float32))
        return total + second, None

    total, _ = lax.scan(matvec_step, jnp.zeros((SECTORS, PAD, PAD), jnp.float32), (left_blocks, right_blocks, shifts))
    product_sum = jnp.where(inside, total, jnp.zeros_like(total))
    corrected = states.astype(jnp.float32) - step_sizes[:, None, None] * product_sum
    update = jnp.where(inside, corrected, jnp.zeros_like(corrected)).astype(jnp.bfloat16)

    def rotate(pieces):
        left, offset = pieces
        ket_block = pick(update, offset)
        pulled = jnp.einsum("sab,sby->say", left.astype(jnp.float32), ket_block.astype(jnp.float32)).astype(jnp.bfloat16)
        rotated = jnp.einsum("sax,say->sxy", update.astype(jnp.float32), pulled.astype(jnp.float32))
        return (rotated * (PAD ** -0.5)).astype(jnp.bfloat16)

    new_left = lax.map(rotate, (left_blocks, shifts))
    return update, new_left
```

```python
import functools

import jax
import jax.numpy as jnp
from jax import lax
from jax.experimental import pallas as pl
from jax.experimental.pallas import tpu as pltpu
from jax.sharding import PartitionSpec as P

MESH = pl.DeviceIdType.MESH
BF16 = jnp.bfloat16
F32 = jnp.float32
NT = (((1,), (1,)), ((), ()))
TN = (((0,), (0,)), ((), ()))
SIDE = 4
CHIPS = SIDE * SIDE
ROWS = 16


def ring_distance(step):
    return min(step, SIDE - step)


OFFSETS = sorted(
    [(dy, dx) for dy in range(SIDE) for dx in range(SIDE) if (dy, dx) != (0, 0)],
    key=lambda o: -(ring_distance(o[0]) + ring_distance(o[1])),
)


def product_kernel(
    shifts, widths, steps, state_hbm, left_hbm, right_hbm,
    upd_out, w_out,
    state, ext0, ext1, left, right, half, total, sibout, sibin, sums, arrived, upd,
    load_sem, left_sem, right_sem, out_sem,
    z1_send, z1_recv, f1_send, f1_recv, sib_send, sib_recv,
    rs_send, rs_recv, ag_send, ag_recv, agf_send, agf_recv,
    z2_send, z2_recv, z2f_send, z2f_recv,
):
    ext = (ext0, ext1)
    sectors = lax.axis_size("sec")
    z = lax.axis_index("sec")
    chan = lax.axis_index("chan")
    core = lax.rem(chan, 2)
    chip = chan // 2
    y, x = chip // SIDE, lax.rem(chip, SIDE)
    sib = chan + 1 - 2 * core
    channels = left_hbm.shape[0]
    pad = state_hbm.shape[1]
    wide = pad // 2

    load = pltpu.make_async_copy(state_hbm.at[0], state, load_sem)
    load.start()
    loads = []
    for c in range(channels):
        copy = pltpu.make_async_copy(left_hbm.at[c, 0], left.at[c], left_sem.at[c])
        copy.start()
        loads.append(copy)
    for j in range(2):
        for c in range(channels):
            copy = pltpu.make_async_copy(
                right_hbm.at[c, 0, :, pl.ds(j * wide, wide)],
                right.at[j, :, pl.ds(c * wide, wide)],
                right_sem.at[j, c],
            )
            copy.start()
            loads.append(copy)

    def peer(dy, dx):
        there = lax.rem(y + dy, SIDE) * SIDE + lax.rem(x + dx, SIDE)
        return there

    barrier = pltpu.get_barrier_semaphore()
    up, down = lax.rem(z + 1, sectors), lax.rem(z + sectors - 1, sectors)
    for target in (up, down):
        pl.semaphore_signal(barrier, 1, device_id=(target, chan), device_id_type=MESH)
    pl.semaphore_signal(barrier, 1, device_id=(z, sib), device_id_type=MESH)
    for dy, dx in OFFSETS:
        pl.semaphore_signal(
            barrier, 1, device_id=(z, peer(dy, dx) * 2 + core), device_id_type=MESH
        )

    load.wait()
    width = widths[0]
    rows_at = lax.broadcasted_iota(jnp.int32, (pad, pad), 0)
    cols_at = lax.broadcasted_iota(jnp.int32, (pad, pad), 1)
    kept = jnp.where((rows_at < width) & (cols_at < width), state[...].astype(F32), 0.0).astype(BF16)
    ext0[1] = kept[:, :wide]
    ext1[1] = kept[:, wide:]

    @pl.when(z == 0)
    def _():
        ext0[0] = jnp.zeros((pad, wide), BF16)
        ext1[0] = jnp.zeros((pad, wide), BF16)
        upd[0] = jnp.zeros((pad, pad), BF16)

    @pl.when(z == sectors - 1)
    def _():
        ext0[2] = jnp.zeros((pad, wide), BF16)
        ext1[2] = jnp.zeros((pad, wide), BF16)
        upd[2] = jnp.zeros((pad, pad), BF16)

    pl.semaphore_wait(barrier, 3 + len(OFFSETS))

    slots = (0, 2)
    can_send = (z < sectors - 1, z > 0)
    can_take = (z > 0, z < sectors - 1)
    targets = (up, down)
    part = pl.ds(pl.multiple_of(core * (wide // 2), wide // 2), wide // 2)
    other = pl.ds(pl.multiple_of((1 - core) * (wide // 2), wide // 2), wide // 2)

    def halo(j, d):
        return pltpu.make_async_remote_copy(
            ext[j].at[1, :, part], ext[j].at[slots[d], :, part],
            z1_send.at[j, d], z1_recv.at[j, d],
            device_id=(targets[d], chan), device_id_type=MESH,
        )

    def handed(j, d, columns):
        return pltpu.make_async_remote_copy(
            ext[j].at[slots[d], :, columns], ext[j].at[slots[d], :, columns],
            f1_send.at[j, d], f1_recv.at[j, d],
            device_id=(z, sib), device_id_type=MESH,
        )

    for j in range(2):
        for d in range(2):
            @pl.when(can_send[d])
            def _():
                halo(j, d).start()
    for copy in loads:
        copy.wait()
    for j in range(2):
        for d in range(2):
            @pl.when(can_take[d])
            def _():
                halo(j, d).wait_recv()
                handed(j, d, part).start()
        for d in range(2):
            @pl.when(can_take[d])
            def _():
                handed(j, d, other).wait_recv()
        for c in range(channels):
            source = ext[j][1 - shifts[c]]
            half[:, pl.ds(c * wide, wide)] = jnp.dot(
                left[c], source, preferred_element_type=F32
            ).astype(BF16)
        for r in range(2):
            value = lax.dot_general(
                half[pl.ds(r * wide, wide), :], right[j], NT, preferred_element_type=F32
            ).reshape(CHIPS // 2, 2, ROWS, pad)
            here = pl.ds(r * CHIPS // 2, CHIPS // 2)
            if j == 0:
                total[here] = value
            else:
                total[here] = total[here] + value
                sibout[here] = total[here, 1 - core].astype(BF16)
                pltpu.make_async_remote_copy(
                    sibout.at[here], sibin.at[here], sib_send.at[r], sib_recv.at[r],
                    device_id=(z, sib), device_id_type=MESH,
                ).start()

    for r in range(2):
        here = pl.ds(r * CHIPS // 2, CHIPS // 2)
        pltpu.make_async_remote_copy(
            sibout.at[here], sibin.at[here], sib_send.at[r], sib_recv.at[r],
            device_id=(z, sib), device_id_type=MESH,
        ).wait()
        pair = total[here, core] + sibin[here].astype(F32)
        sums[here] = pair.astype(BF16)
        total[here, core] = pair

    def scattered(i):
        dy, dx = OFFSETS[i]
        there = peer(dy, dx)
        return pltpu.make_async_remote_copy(
            sums.at[there], arrived.at[i], rs_send.at[i], rs_recv.at[i],
            device_id=(z, there * 2 + core), device_id_type=MESH,
        )

    for i in range(len(OFFSETS)):
        scattered(i).start()
    acc = total[chip, core]
    for i in reversed(range(len(OFFSETS))):
        scattered(i).wait_recv()
        acc = acc + arrived[i].astype(F32)

    first = pl.multiple_of(chan * ROWS, ROWS)
    mine = pl.ds(first, ROWS)
    row_ids = first + lax.broadcasted_iota(jnp.int32, (ROWS, pad), 0)
    col_ids = lax.broadcasted_iota(jnp.int32, (ROWS, pad), 1)
    before = jnp.concatenate([ext0[1, mine, :], ext1[1, mine, :]], axis=1).astype(F32)
    corrected = jnp.where((row_ids < width) & (col_ids < width), before - steps[0] * acc, 0.0)
    upd[1, mine, :] = corrected.astype(BF16)

    def rows_of(where, parity):
        return pl.ds(pl.multiple_of((where * 2 + parity) * ROWS, ROWS), ROWS)

    def origin(i):
        if i == len(OFFSETS):
            return chip
        dy, dx = OFFSETS[i]
        return peer(SIDE - dy, SIDE - dx)

    def gathered(i, where):
        dy, dx = OFFSETS[i]
        rows = rows_of(where, core)
        return pltpu.make_async_remote_copy(
            upd.at[1, rows], upd.at[1, rows], ag_send.at[i], ag_recv.at[i],
            device_id=(z, peer(dy, dx) * 2 + core), device_id_type=MESH,
        )

    def to_sibling(i, parity):
        rows = rows_of(origin(i), parity)
        return pltpu.make_async_remote_copy(
            upd.at[1, rows], upd.at[1, rows], agf_send.at[i], agf_recv.at[i],
            device_id=(z, sib), device_id_type=MESH,
        )

    def over_z(i, d):
        rows = rows_of(origin(i), core)
        return pltpu.make_async_remote_copy(
            upd.at[1, rows], upd.at[slots[d], rows], z2_send.at[d, i], z2_recv.at[d, i],
            device_id=(targets[d], chan), device_id_type=MESH,
        )

    def pass_on(i):
        to_sibling(i, core).start()
        for d in range(2):
            @pl.when(can_send[d])
            def _():
                over_z(i, d).start()

    for i in range(len(OFFSETS)):
        gathered(i, chip).start()
    pass_on(len(OFFSETS))
    for i in reversed(range(len(OFFSETS))):
        gathered(i, origin(i)).wait_recv()
        pass_on(i)
    for i in range(len(OFFSETS) + 1):
        to_sibling(i, 1 - core).wait_recv()

    turned = upd[1].T
    outs = []
    for c in range(channels):
        left[c] = jnp.dot(turned, left[c], preferred_element_type=F32).astype(BF16)
        copy = pltpu.make_async_copy(left.at[c], w_out.at[c], out_sem.at[c])
        copy.start()
        outs.append(copy)
    own = pltpu.make_async_copy(upd.at[1], upd_out.at[1], out_sem.at[channels])
    own.start()
    outs.append(own)

    def halo_handed(i, d, parity):
        rows = rows_of(origin(i), parity)
        return pltpu.make_async_remote_copy(
            upd.at[slots[d], rows], upd.at[slots[d], rows], z2f_send.at[d, i], z2f_recv.at[d, i],
            device_id=(z, sib), device_id_type=MESH,
        )

    order = [len(OFFSETS)] + list(reversed(range(len(OFFSETS))))
    for i in order:
        for d in range(2):
            @pl.when(can_take[d])
            def _():
                over_z(i, d).wait_recv()
                halo_handed(i, d, core).start()
    for i in order:
        for d in range(2):
            @pl.when(can_take[d])
            def _():
                halo_handed(i, d, 1 - core).wait_recv()
    for d in range(2):
        copy = pltpu.make_async_copy(
            upd.at[slots[d]], upd_out.at[slots[d]], out_sem.at[channels + 1 + d]
        )
        copy.start()
        outs.append(copy)

    for j in range(2):
        for d in range(2):
            @pl.when(can_send[d])
            def _():
                halo(j, d).wait_send()

            @pl.when(can_take[d])
            def _():
                handed(j, d, part).wait_send()
    for i in range(len(OFFSETS)):
        scattered(i).wait_send()
        gathered(i, chip).wait_send()
    for i in range(len(OFFSETS) + 1):
        to_sibling(i, core).wait_send()
        for d in range(2):
            @pl.when(can_send[d])
            def _():
                over_z(i, d).wait_send()

            @pl.when(can_take[d])
            def _():
                halo_handed(i, d, core).wait_send()
    for copy in outs:
        copy.wait()


def rotate_kernel(shifts, first, scale, w_ref, upd_ref, rows_ref, out_ref):
    channel = pl.program_id(0)
    source = upd_ref[1 - shifts[channel]]
    out_ref[0, 0] = (jnp.dot(w_ref[0], source, preferred_element_type=F32) * scale).astype(BF16)

    @pl.when(channel == 0)
    def _():
        rows_ref[0] = upd_ref[1, pl.ds(pl.multiple_of(first[0], ROWS), ROWS), :]


def shards(state_blocks, left_blocks, right_blocks, widths, step_sizes, shifts):
    channels, _, pad, _ = left_blocks.shape
    wide = pad // 2
    n = len(OFFSETS)
    smem = pl.BlockSpec(memory_space=pltpu.SMEM)
    hbm = pl.BlockSpec(memory_space=pl.ANY)
    dma = pltpu.SemaphoreType.DMA
    upd, turned = pl.pallas_call(
        product_kernel,
        name="product",
        out_shape=(
            jax.ShapeDtypeStruct((3, pad, pad), BF16),
            jax.ShapeDtypeStruct((channels, pad, pad), BF16),
        ),
        in_specs=[smem] * 3 + [hbm] * 3,
        out_specs=(hbm, hbm),
        scratch_shapes=[
            pltpu.VMEM((pad, pad), BF16),
            pltpu.VMEM((3, pad, wide), BF16),
            pltpu.VMEM((3, pad, wide), BF16),
            pltpu.VMEM((channels, pad, pad), BF16),
            pltpu.VMEM((2, pad, channels * wide), BF16),
            pltpu.VMEM((pad, channels * wide), BF16),
            pltpu.VMEM((CHIPS, 2, ROWS, pad), F32),
            pltpu.VMEM((CHIPS, ROWS, pad), BF16),
            pltpu.VMEM((CHIPS, ROWS, pad), BF16),
            pltpu.VMEM((CHIPS, ROWS, pad), BF16),
            pltpu.VMEM((n, ROWS, pad), BF16),
            pltpu.VMEM((3, pad, pad), BF16),
            dma(()), dma((channels,)), dma((2, channels)), dma((channels + 3,)),
            dma((2, 2)), dma((2, 2)), dma((2, 2)), dma((2, 2)), dma((2,)), dma((2,)),
            dma((n,)), dma((n,)), dma((n,)), dma((n,)), dma((n + 1,)), dma((n + 1,)),
            dma((2, n + 1)), dma((2, n + 1)), dma((2, n + 1)), dma((2, n + 1)),
        ],
        compiler_params=pltpu.CompilerParams(
            collective_id=0, has_side_effects=True, vmem_limit_bytes=32 << 20
        ),
        cost_estimate=pl.CostEstimate(flops=6 << 30, bytes_accessed=16 << 20, transcendentals=0),
    )(shifts, widths, step_sizes, state_blocks, left_blocks, right_blocks)

    first = (lax.axis_index("chan") * ROWS).astype(jnp.int32).reshape(1)
    rows, new_left = pl.pallas_call(
        lambda s, f, *refs: rotate_kernel(s, f, pad ** (-0.5), *refs),
        name="rotate",
        out_shape=(
            jax.ShapeDtypeStruct((1, ROWS, pad), BF16),
            jax.ShapeDtypeStruct((channels, 1, pad, pad), BF16),
        ),
        grid_spec=pltpu.PrefetchScalarGridSpec(
            num_scalar_prefetch=2,
            grid=(channels,),
            in_specs=[
                pl.BlockSpec((1, pad, pad), lambda c, s, f: (c, 0, 0)),
                pl.BlockSpec((3, pad, pad), lambda c, s, f: (0, 0, 0)),
            ],
            out_specs=(
                pl.BlockSpec((1, ROWS, pad), lambda c, s, f: (0, 0, 0)),
                pl.BlockSpec((1, 1, pad, pad), lambda c, s, f: (c, 0, 0, 0)),
            ),
        ),
        compiler_params=pltpu.CompilerParams(vmem_limit_bytes=16 << 20),
        cost_estimate=pl.CostEstimate(flops=2 << 30, bytes_accessed=10 << 20, transcendentals=0),
    )(shifts, first, turned, upd)
    return rows, new_left


def solution(mesh):
    placed = (
        P("sec", None, None),
        P("chan", "sec", None, None),
        P("chan", "sec", None, None),
        P("sec"),
        P("sec"),
        P("chan"),
    )
    return jax.shard_map(
        shards,
        mesh=mesh,
        in_specs=placed,
        out_specs=(P("sec", "chan", None), P("chan", "sec", None, None)),
        check_vma=False,
    )
```

```python
import functools

import jax
import jax.numpy as jnp
from jax import lax
from jax.experimental import pallas as pl
from jax.experimental.pallas import tpu as pltpu
from jax.sharding import PartitionSpec as P

MESH = pl.DeviceIdType.MESH
BF16 = jnp.bfloat16
F32 = jnp.float32
NT = (((1,), (1,)), ((), ()))
SIDE = 4
CHIPS = SIDE * SIDE
ROWS = 16


def ring_distance(step):
    return min(step, SIDE - step)


OFFSETS = sorted(
    [(dy, dx) for dy in range(SIDE) for dx in range(SIDE) if (dy, dx) != (0, 0)],
    key=lambda o: -(ring_distance(o[0]) + ring_distance(o[1])),
)


GROUPS = [(0, 0), (0, 1), (0, 3), (0, 2), (1, None), (3, None), (2, None)]


def product_kernel(
    shifts, widths, steps, state_hbm, left_hbm, right_hbm,
    upd, w_out,
    state, ext0, ext1, left, right, half, total, sibout, sibin, sums, arrived,
    load_sem, z1_send, z1_recv, f1_send, f1_recv, sib_send, sib_recv,
    rs_send, rs_recv, ag_send, ag_recv, agf_send, agf_recv,
    z2_send, z2_recv, z2f_send, z2f_recv,
):
    ext = (ext0, ext1)
    sectors = lax.axis_size("sec")
    z = lax.axis_index("sec")
    chan = lax.axis_index("chan")
    core = lax.rem(chan, 2)
    chip = chan // 2
    y, x = chip // SIDE, lax.rem(chip, SIDE)
    sib = chan + 1 - 2 * core
    channels = left_hbm.shape[0]
    pad = state_hbm.shape[1]
    wide = pad // 2
    up, down = lax.rem(z + 1, sectors), lax.rem(z + sectors - 1, sectors)

    def peer(dy, dx):
        return lax.rem(y + dy, SIDE) * SIDE + lax.rem(x + dx, SIDE)

    def remote(src, dst, send, recv, where, there):
        return pltpu.make_async_remote_copy(
            src, dst, send, recv, device_id=(where, there), device_id_type=MESH
        )

    def wait_bytes(ref, sem):
        pltpu.make_async_copy(ref, ref, sem).wait()

    load = pltpu.make_async_copy(state_hbm.at[0], state, load_sem.at[0])
    load.start()
    barrier = pltpu.get_barrier_semaphore()
    for target in (up, down):
        pl.semaphore_signal(barrier, 1, device_id=(target, chan), device_id_type=MESH)
    for dy, dx in OFFSETS:
        pl.semaphore_signal(
            barrier, 1, device_id=(z, peer(dy, dx) * 2 + core), device_id_type=MESH
        )
    pl.semaphore_signal(barrier, 1, device_id=(z, sib), device_id_type=MESH)

    load.wait()
    width = widths[0]
    rows_at = lax.broadcasted_iota(jnp.int32, (pad, wide), 0)
    cols_at = lax.broadcasted_iota(jnp.int32, (pad, wide), 1)
    for j in range(2):
        kept = (rows_at < width) & (cols_at < width - j * wide)
        values = state[:, pl.ds(j * wide, wide)].astype(F32)
        ext[j][1] = jnp.where(kept, values, 0.0).astype(BF16)

    slots = (0, 2)
    can_send = (z < sectors - 1, z > 0)
    can_take = (z > 0, z < sectors - 1)
    targets = (up, down)
    part = pl.ds(pl.multiple_of(core * wide, wide), wide)
    other = pl.ds(pl.multiple_of((1 - core) * wide, wide), wide)

    def halo(j, d):
        return remote(
            ext[j].at[1, part], ext[j].at[slots[d], part],
            z1_send.at[j, d], z1_recv.at[j, d], targets[d], chan,
        )

    def handed(j, d, rows):
        return remote(
            ext[j].at[slots[d], rows], ext[j].at[slots[d], rows],
            f1_send.at[j, d], f1_recv.at[j, d], z, sib,
        )

    pl.semaphore_wait(barrier, 3 + len(OFFSETS))
    for j in range(2):
        for d in range(2):
            pl.when(can_send[d])(halo(j, d).start)
    loads = [pltpu.make_async_copy(left_hbm.at[:, 0], left, load_sem.at[1])]
    for j in range(2):
        loads.append(
            pltpu.make_async_copy(
                right_hbm.at[:, 0, :, pl.ds(j * wide, wide)], right.at[j], load_sem.at[2 + j]
            )
        )
    for copy in loads:
        copy.start()

    @pl.when(z == 0)
    def _():
        ext0[0] = jnp.zeros((pad, wide), BF16)
        ext1[0] = jnp.zeros((pad, wide), BF16)
        upd[0] = jnp.zeros(upd.shape[1:], BF16)

    @pl.when(z == sectors - 1)
    def _():
        ext0[2] = jnp.zeros((pad, wide), BF16)
        ext1[2] = jnp.zeros((pad, wide), BF16)
        upd[2] = jnp.zeros(upd.shape[1:], BF16)

    for copy in loads:
        copy.wait()

    def hand_over(j):
        for d in range(2):
            @pl.when(can_take[d])
            def _():
                halo(j, d).wait_recv()
                handed(j, d, part).start()

    def pair_sent(r):
        here = pl.ds(r * CHIPS // 2, CHIPS // 2)
        return remote(sibout.at[here], sibin.at[here], sib_send.at[r], sib_recv.at[r], z, sib)

    hand_over(0)
    for j in range(2):
        for d in range(2):
            pl.when(can_take[d])(handed(j, d, other).wait_recv)
        for c in range(channels):
            source = ext[j][1 - shifts[c]]
            half[:, pl.ds(c * wide, wide)] = jnp.dot(
                left[c], source, preferred_element_type=F32
            ).astype(BF16)
        for r in range(2):
            beside = jnp.concatenate([right[j, c] for c in range(channels)], axis=1)
            value = lax.dot_general(
                half[pl.ds(r * wide, wide), :], beside, NT, preferred_element_type=F32
            ).reshape(CHIPS // 2, 2, ROWS, pad)
            here = pl.ds(r * CHIPS // 2, CHIPS // 2)
            if j == 0:
                total[here] = value
                if r == 0:
                    hand_over(1)
            else:
                total[here] = total[here] + value
                sibout[here] = total[here, 1 - core].astype(BF16)
                pair_sent(r).start()

    for r in range(2):
        here = pl.ds(r * CHIPS // 2, CHIPS // 2)
        pair_sent(r).wait_recv()
        pair = total[here, core] + sibin[here].astype(F32)
        sums[here] = pair.astype(BF16)
        total[here, core] = pair
    for i, (dy, dx) in enumerate(OFFSETS):
        there = peer(dy, dx)
        remote(sums.at[there], arrived.at[i], rs_send, rs_recv, z, there * 2 + core).start()

    for j in range(2):
        for d in range(2):
            pl.when(can_send[d])(halo(j, d).wait_send)
            pl.when(can_take[d])(handed(j, d, part).wait_send)
        pair_sent(j).wait_send()

    first = pl.multiple_of(chan * ROWS, ROWS)
    mine = pl.ds(first, ROWS)
    row_ids = first + lax.broadcasted_iota(jnp.int32, (ROWS, pad), 0)
    col_ids = lax.broadcasted_iota(jnp.int32, (ROWS, pad), 1)
    before = jnp.concatenate([ext0[1, mine, :], ext1[1, mine, :]], axis=1).astype(F32)
    acc = total[chip, core]
    wait_bytes(arrived, rs_recv)
    for i in range(len(OFFSETS)):
        acc = acc + arrived[i].astype(F32)
    corrected = jnp.where((row_ids < width) & (col_ids < width), before - steps[0] * acc, 0.0)
    upd[1, chip, core] = corrected.astype(BF16)

    def group(slot, g, parity):
        gy, gx = GROUPS[g]
        if gx is None:
            rows = pl.ds(pl.multiple_of(lax.rem(y + gy, SIDE) * SIDE, SIDE), SIDE)
            return upd.at[slot, rows, parity]
        return upd.at[slot, peer(gy, gx), parity]

    def gathered(i, where):
        dy, dx = OFFSETS[i]
        block = upd.at[1, where, core]
        return remote(block, block, ag_send, ag_recv.at[i], z, peer(dy, dx) * 2 + core)

    def take(gy, gx):
        i = OFFSETS.index(((SIDE - gy) % SIDE, (SIDE - gx) % SIDE))
        gathered(i, peer(gy, gx)).wait_recv()

    def to_sibling(g, parity):
        block = group(1, g, parity)
        return remote(block, block, agf_send.at[g], agf_recv.at[g], z, sib)

    def over_z(g, d):
        return remote(
            group(1, g, core), group(slots[d], g, core),
            z2_send.at[d, g], z2_recv.at[d, g], targets[d], chan,
        )

    def z_on(g):
        for d in range(2):
            pl.when(can_send[d])(over_z(g, d).start)

    z_on(0)
    for i in range(len(OFFSETS)):
        gathered(i, chip).start()
    to_sibling(0, core).start()
    for g in range(1, len(GROUPS)):
        gy, gx = GROUPS[g]
        for taken in range(SIDE) if gx is None else (gx,):
            take(gy, taken)
        z_on(g)
        to_sibling(g, core).start()
    wait_bytes(arrived, rs_send)
    wait_bytes(arrived, ag_send)
    for g in range(len(GROUPS)):
        to_sibling(g, 1 - core).wait_recv()

    def halo_handed(gy, d, parity):
        rows = pl.ds(pl.multiple_of(lax.rem(y + gy, SIDE) * SIDE, SIDE), SIDE)
        block = upd.at[slots[d], rows, parity]
        return remote(block, block, z2f_send.at[d, gy], z2f_recv.at[d, gy], z, sib)

    def hand_row(gy):
        for d in range(2):
            @pl.when(can_take[d])
            def _():
                for g in range(len(GROUPS)):
                    if GROUPS[g][0] == gy:
                        over_z(g, d).wait_recv()
                halo_handed(gy, d, core).start()

    hand_row(0)
    turned = upd[1].reshape(pad, pad).T
    for c in range(channels):
        if c == channels // 2:
            hand_row(1)
            hand_row(3)
        w_out[c] = jnp.dot(turned, left[c], preferred_element_type=F32).astype(BF16)
    hand_row(2)
    for g in range(len(GROUPS)):
        to_sibling(g, core).wait_send()
        for d in range(2):
            pl.when(can_send[d])(over_z(g, d).wait_send)
    for gy in range(SIDE):
        for d in range(2):
            @pl.when(can_take[d])
            def _():
                halo_handed(gy, d, core).wait_send()
                halo_handed(gy, d, 1 - core).wait_recv()


def rotate_kernel(scale, shifts, w, upd, rows_out, out, done, sem):
    channels, pad, _ = w.shape
    chan = lax.axis_index("chan")
    rows = pltpu.make_async_copy(
        upd.at[1, chan // 2, lax.rem(chan, 2)], rows_out.at[0], sem.at[channels]
    )
    rows.start()
    copies = [pltpu.make_async_copy(done.at[c], out.at[c, 0], sem.at[c]) for c in range(channels)]
    for c in range(channels):
        source = upd[1 - shifts[c]].reshape(pad, pad)
        done[c] = (jnp.dot(w[c], source, preferred_element_type=F32) * scale).astype(BF16)
        copies[c].start()
    rows.wait()
    for copy in copies:
        copy.wait()


def shards(state_blocks, left_blocks, right_blocks, widths, step_sizes, shifts):
    channels, _, pad, _ = left_blocks.shape
    wide = pad // 2
    n, m = len(OFFSETS), len(GROUPS)
    smem = pl.BlockSpec(memory_space=pltpu.SMEM)
    hbm = pl.BlockSpec(memory_space=pltpu.HBM)
    vmem = pl.BlockSpec(memory_space=pltpu.VMEM)
    dma = pltpu.SemaphoreType.DMA
    blocks = (pltpu.with_memory_space_constraint(a, pltpu.HBM) for a in (state_blocks, left_blocks, right_blocks))
    upd, turned = pl.pallas_call(
        product_kernel,
        name="product",
        out_shape=(
            jax.ShapeDtypeStruct((3, CHIPS, 2, ROWS, pad), BF16),
            jax.ShapeDtypeStruct((channels, pad, pad), BF16),
        ),
        in_specs=[smem] * 3 + [hbm] * 3,
        out_specs=(vmem, vmem),
        scratch_shapes=[
            pltpu.VMEM((pad, pad), BF16),
            pltpu.VMEM((3, pad, wide), BF16),
            pltpu.VMEM((3, pad, wide), BF16),
            pltpu.VMEM((channels, pad, pad), BF16),
            pltpu.VMEM((2, channels, pad, wide), BF16),
            pltpu.VMEM((pad, channels * wide), BF16),
            pltpu.VMEM((CHIPS, 2, ROWS, pad), F32),
            pltpu.VMEM((CHIPS, ROWS, pad), BF16),
            pltpu.VMEM((CHIPS, ROWS, pad), BF16),
            pltpu.VMEM((CHIPS, ROWS, pad), BF16),
            pltpu.VMEM((n, ROWS, pad), BF16),
            dma((4,)), dma((2, 2)), dma((2, 2)), dma((2, 2)), dma((2, 2)), dma((2,)), dma((2,)),
            dma(()), dma(()), dma(()), dma((n,)), dma((m,)), dma((m,)),
            dma((2, m)), dma((2, m)), dma((2, SIDE)), dma((2, SIDE)),
        ],
        compiler_params=pltpu.CompilerParams(
            collective_id=0, has_side_effects=True, vmem_limit_bytes=32 << 20
        ),
        cost_estimate=pl.CostEstimate(flops=6 << 30, bytes_accessed=16 << 20, transcendentals=0),
    )(shifts, widths, step_sizes, *blocks)

    rows, new_left = pl.pallas_call(
        functools.partial(rotate_kernel, pad ** (-0.5)),
        name="rotate",
        out_shape=(
            jax.ShapeDtypeStruct((1, ROWS, pad), BF16),
            jax.ShapeDtypeStruct((channels, 1, pad, pad), BF16),
        ),
        in_specs=[smem, vmem, vmem],
        out_specs=(hbm, hbm),
        scratch_shapes=[
            pltpu.VMEM((channels, pad, pad), BF16),
            dma((channels + 1,)),
        ],
        compiler_params=pltpu.CompilerParams(vmem_limit_bytes=16 << 20),
        cost_estimate=pl.CostEstimate(flops=2 << 30, bytes_accessed=10 << 20, transcendentals=0),
    )(shifts, turned, upd)
    return rows, new_left


def solution(mesh):
    placed = (
        P("sec", None, None),
        P("chan", "sec", None, None),
        P("chan", "sec", None, None),
        P("sec"),
        P("sec"),
        P("chan"),
    )
    return jax.shard_map(
        shards,
        mesh=mesh,
        in_specs=placed,
        out_specs=(P("sec", "chan", None), P("chan", "sec", None, None)),
        check_vma=False,
    )
```

```python
import functools

import jax
import jax.numpy as jnp
from jax import lax
from jax.experimental import pallas as pl
from jax.experimental.pallas import tpu as pltpu
from jax.sharding import PartitionSpec as P

MESH = pl.DeviceIdType.MESH
BF16 = jnp.bfloat16
F32 = jnp.float32
NT = (((1,), (1,)), ((), ()))
SIDE = 4
CHIPS = SIDE * SIDE
ROWS = 16


def ring_distance(step):
    return min(step, SIDE - step)


OFFSETS = sorted(
    [(dy, dx) for dy in range(SIDE) for dx in range(SIDE) if (dy, dx) != (0, 0)],
    key=lambda o: -(ring_distance(o[0]) + ring_distance(o[1])),
)


GROUPS = [(0, 0)] + list(reversed(OFFSETS))
SENT = list(range(len(OFFSETS) - SIDE, len(OFFSETS))) + list(range(len(OFFSETS) - SIDE))


def product_kernel(
    shifts, widths, steps, state_hbm, left_hbm, right_hbm,
    upd, w_out,
    state, ext0, ext1, left, right, half, total, sibout, sibin, sums, arrived,
    load_sem, z1_recv, f1_recv, sib_recv, rs_recv, ag_recv, agf_recv, z2_recv, z2f_recv,
    early_send, sib_send, rs_send, ag_send, agf_send, z2_send, z2f_send,
):
    ext = (ext0, ext1)
    sectors = lax.axis_size("sec")
    z = lax.axis_index("sec")
    chan = lax.axis_index("chan")
    core = lax.rem(chan, 2)
    chip = chan // 2
    y, x = chip // SIDE, lax.rem(chip, SIDE)
    sib = chan + 1 - 2 * core
    channels = left_hbm.shape[0]
    pad = state_hbm.shape[1]
    wide = pad // 2
    up, down = lax.rem(z + 1, sectors), lax.rem(z + sectors - 1, sectors)

    def peer(dy, dx):
        return lax.rem(y + dy, SIDE) * SIDE + lax.rem(x + dx, SIDE)

    def remote(src, dst, send, recv, where, there):
        return pltpu.make_async_remote_copy(
            src, dst, send, recv, device_id=(where, there), device_id_type=MESH
        )

    def wait_bytes(ref, sem):
        pltpu.make_async_copy(ref, ref, sem).wait()

    load = pltpu.make_async_copy(state_hbm.at[0], state, load_sem.at[0])
    load.start()
    barrier = pltpu.get_barrier_semaphore()
    for target in (up, down):
        pl.semaphore_signal(barrier, 1, device_id=(target, chan), device_id_type=MESH)
    for dy, dx in OFFSETS:
        pl.semaphore_signal(
            barrier, 1, device_id=(z, peer(dy, dx) * 2 + core), device_id_type=MESH
        )
    pl.semaphore_signal(barrier, 1, device_id=(z, sib), device_id_type=MESH)

    load.wait()
    width = widths[0]
    rows_at = lax.broadcasted_iota(jnp.int32, (pad, wide), 0)
    cols_at = lax.broadcasted_iota(jnp.int32, (pad, wide), 1)
    for j in range(2):
        kept = (rows_at < width) & (cols_at < width - j * wide)
        values = state[:, pl.ds(j * wide, wide)].astype(F32)
        ext[j][1] = jnp.where(kept, values, 0.0).astype(BF16)

    slots = (0, 2)
    targets = (up, down)
    sent_slot = (jnp.where(z == sectors - 1, 3, 1), jnp.where(z == 0, 3, 1))

    @pl.when((z == 0) | (z == sectors - 1))
    def _():
        ext0[3] = jnp.zeros((pad, wide), BF16)
        ext1[3] = jnp.zeros((pad, wide), BF16)
        upd[3] = jnp.zeros(upd.shape[1:], BF16)

    part = pl.ds(pl.multiple_of(core * wide, wide), wide)
    other = pl.ds(pl.multiple_of((1 - core) * wide, wide), wide)

    def halo(j, d):
        return remote(
            ext[j].at[sent_slot[d], part], ext[j].at[slots[d], part],
            early_send, z1_recv.at[j, d], targets[d], chan,
        )

    def handed(j, d, rows):
        return remote(
            ext[j].at[slots[d], rows], ext[j].at[slots[d], rows],
            early_send, f1_recv.at[j, d], z, sib,
        )

    pl.semaphore_wait(barrier, 3 + len(OFFSETS))
    for j in range(2):
        for d in range(2):
            halo(j, d).start()
    loads = [pltpu.make_async_copy(left_hbm.at[:, 0], left, load_sem.at[1])]
    for j in range(2):
        loads.append(
            pltpu.make_async_copy(
                right_hbm.at[:, 0, :, pl.ds(j * wide, wide)], right.at[j], load_sem.at[2 + j]
            )
        )
    for copy in loads:
        copy.start()

    for copy in loads:
        copy.wait()

    def hand_over(j):
        for d in range(2):
            halo(j, d).wait_recv()
            handed(j, d, part).start()

    def pair_sent(r):
        here = pl.ds(r * CHIPS // 2, CHIPS // 2)
        return remote(sibout.at[here], sibin.at[here], sib_send, sib_recv.at[r], z, sib)

    hand_over(0)
    for j in range(2):
        for d in range(2):
            handed(j, d, other).wait_recv()
        for c in range(channels):
            source = ext[j][1 - shifts[c]]
            half[:, pl.ds(c * wide, wide)] = jnp.dot(
                left[c], source, preferred_element_type=F32
            ).astype(BF16)
        for r in range(2):
            beside = jnp.concatenate([right[j, c] for c in range(channels)], axis=1)
            value = lax.dot_general(
                half[pl.ds(r * wide, wide), :], beside, NT, preferred_element_type=F32
            ).reshape(CHIPS // 2, 2, ROWS, pad)
            here = pl.ds(r * CHIPS // 2, CHIPS // 2)
            if j == 0:
                total[here] = value
                if r == 0:
                    hand_over(1)
            else:
                total[here] = total[here] + value
                sibout[here] = total[here, 1 - core].astype(BF16)
                pair_sent(r).start()

    for r in range(2):
        here = pl.ds(r * CHIPS // 2, CHIPS // 2)
        pair_sent(r).wait_recv()
        pair = total[here, core] + sibin[here].astype(F32)
        sums[here] = pair.astype(BF16)
        total[here, core] = pair
    for i, (dy, dx) in enumerate(OFFSETS):
        there = peer(dy, dx)
        remote(sums.at[there], arrived.at[i], rs_send, rs_recv, z, there * 2 + core).start()

    first = pl.multiple_of(chan * ROWS, ROWS)
    mine = pl.ds(first, ROWS)
    row_ids = first + lax.broadcasted_iota(jnp.int32, (ROWS, pad), 0)
    col_ids = lax.broadcasted_iota(jnp.int32, (ROWS, pad), 1)
    before = jnp.concatenate([ext0[1, mine, :], ext1[1, mine, :]], axis=1).astype(F32)
    acc = total[chip, core]
    wait_bytes(arrived, rs_recv)
    for i in range(len(OFFSETS)):
        acc = acc + arrived[i].astype(F32)
    corrected = jnp.where((row_ids < width) & (col_ids < width), before - steps[0] * acc, 0.0)
    upd[1, chip, core] = corrected.astype(BF16)

    def group(slot, g, parity):
        return upd.at[slot, peer(*GROUPS[g]), parity]

    def gathered(i, where):
        dy, dx = OFFSETS[i]
        block = upd.at[1, where, core]
        return remote(block, block, ag_send, ag_recv.at[i], z, peer(dy, dx) * 2 + core)

    def take(gy, gx):
        i = OFFSETS.index(((SIDE - gy) % SIDE, (SIDE - gx) % SIDE))
        gathered(i, peer(gy, gx)).wait_recv()

    def to_sibling(g, parity):
        block = group(1, g, parity)
        return remote(block, block, agf_send, agf_recv, z, sib)

    def over_z(g, d):
        return remote(
            group(sent_slot[d], g, core), group(slots[d], g, core),
            z2_send, z2_recv.at[d, GROUPS[g][0]], targets[d], chan,
        )

    def z_on(g):
        for d in range(2):
            over_z(g, d).start()

    z_on(0)
    for i in SENT:
        gathered(i, chip).start()
    to_sibling(0, core).start()
    for g in range(1, len(GROUPS)):
        take(*GROUPS[g])
        z_on(g)
        to_sibling(g, core).start()
    wait_bytes(upd.at[1, :, 1 - core], agf_recv)

    def chip_row(gy, d, parity):
        rows = pl.ds(pl.multiple_of(lax.rem(y + gy, SIDE) * SIDE, SIDE), SIDE)
        return upd.at[slots[d], rows, parity]

    def hand_row(gy):
        for d in range(2):
            block = chip_row(gy, d, core)
            wait_bytes(block, z2_recv.at[d, gy])
            remote(block, block, z2f_send, z2f_recv, z, sib).start()

    hand_row(0)
    turned = upd[1].reshape(pad, pad).T
    for c in range(channels):
        if c == channels // 2:
            hand_row(1)
            hand_row(3)
        w_out[c] = jnp.dot(turned, left[c], preferred_element_type=F32).astype(BF16)
    hand_row(2)
    for sem, ref in (
        (early_send, left.at[pl.ds(0, 2)]),
        (sib_send, sibout),
        (rs_send, arrived),
        (ag_send, arrived),
        (agf_send, sums),
        (z2_send, upd.at[0]),
        (z2f_send, upd.at[0]),
    ):
        wait_bytes(ref, sem)
    wait_bytes(upd.at[0], z2f_recv)


def rotate_kernel(scale, shifts, w, upd, rows_out, out, done, sem):
    channels, pad, _ = w.shape
    chan = lax.axis_index("chan")
    rows = pltpu.make_async_copy(
        upd.at[1, chan // 2, lax.rem(chan, 2)], rows_out.at[0], sem.at[channels]
    )
    rows.start()
    copies = [pltpu.make_async_copy(done.at[c], out.at[c, 0], sem.at[c]) for c in range(channels)]
    for c in range(channels):
        source = upd[1 - shifts[c]].reshape(pad, pad)
        done[c] = (jnp.dot(w[c], source, preferred_element_type=F32) * scale).astype(BF16)
        copies[c].start()
    rows.wait()
    for copy in copies:
        copy.wait()


def shards(state_blocks, left_blocks, right_blocks, widths, step_sizes, shifts):
    channels, _, pad, _ = left_blocks.shape
    wide = pad // 2
    n = len(OFFSETS)
    smem = pl.BlockSpec(memory_space=pltpu.SMEM)
    hbm = pl.BlockSpec(memory_space=pltpu.HBM)
    vmem = pl.BlockSpec(memory_space=pltpu.VMEM)
    dma = pltpu.SemaphoreType.DMA
    blocks = (pltpu.with_memory_space_constraint(a, pltpu.HBM) for a in (state_blocks, left_blocks, right_blocks))
    upd, turned = pl.pallas_call(
        product_kernel,
        name="product",
        out_shape=(
            jax.ShapeDtypeStruct((4, CHIPS, 2, ROWS, pad), BF16),
            jax.ShapeDtypeStruct((channels, pad, pad), BF16),
        ),
        in_specs=[smem] * 3 + [hbm] * 3,
        out_specs=(vmem, vmem),
        scratch_shapes=[
            pltpu.VMEM((pad, pad), BF16),
            pltpu.VMEM((4, pad, wide), BF16),
            pltpu.VMEM((4, pad, wide), BF16),
            pltpu.VMEM((channels, pad, pad), BF16),
            pltpu.VMEM((2, channels, pad, wide), BF16),
            pltpu.VMEM((pad, channels * wide), BF16),
            pltpu.VMEM((CHIPS, 2, ROWS, pad), F32),
            pltpu.VMEM((CHIPS, ROWS, pad), BF16),
            pltpu.VMEM((CHIPS, ROWS, pad), BF16),
            pltpu.VMEM((CHIPS, ROWS, pad), BF16),
            pltpu.VMEM((n, ROWS, pad), BF16),
            dma((4,)), dma((2, 2)), dma((2, 2)), dma((2,)), dma(()), dma((n,)), dma(()), dma((2, SIDE)), dma(()),
            *[dma(())] * 7,
        ],
        compiler_params=pltpu.CompilerParams(
            collective_id=0, has_side_effects=True, vmem_limit_bytes=32 << 20
        ),
        cost_estimate=pl.CostEstimate(flops=6 << 30, bytes_accessed=16 << 20, transcendentals=0),
    )(shifts, widths, step_sizes, *blocks)

    rows, new_left = pl.pallas_call(
        functools.partial(rotate_kernel, pad ** (-0.5)),
        name="rotate",
        out_shape=(
            jax.ShapeDtypeStruct((1, ROWS, pad), BF16),
            jax.ShapeDtypeStruct((channels, 1, pad, pad), BF16),
        ),
        in_specs=[smem, vmem, vmem],
        out_specs=(hbm, hbm),
        scratch_shapes=[
            pltpu.VMEM((channels, pad, pad), BF16),
            dma((channels + 1,)),
        ],
        compiler_params=pltpu.CompilerParams(vmem_limit_bytes=16 << 20),
        cost_estimate=pl.CostEstimate(flops=2 << 30, bytes_accessed=10 << 20, transcendentals=0),
    )(shifts, turned, upd)
    return rows, new_left


def solution(mesh):
    placed = (
        P("sec", None, None),
        P("chan", "sec", None, None),
        P("chan", "sec", None, None),
        P("sec"),
        P("sec"),
        P("chan"),
    )
    return jax.shard_map(
        shards,
        mesh=mesh,
        in_specs=placed,
        out_specs=(P("sec", "chan", None), P("chan", "sec", None, None)),
        check_vma=False,
    )
```

```python
import functools

import jax
import jax.numpy as jnp
from jax import lax
from jax.experimental import pallas as pl
from jax.experimental.pallas import tpu as pltpu
from jax.sharding import PartitionSpec as P

MESH = pl.DeviceIdType.MESH
BF16 = jnp.bfloat16
F32 = jnp.float32
NT = (((1,), (1,)), ((), ()))
SIDE = 4
CHIPS = SIDE * SIDE
ROWS = 16


def ring_distance(step):
    return min(step, SIDE - step)


OFFSETS = sorted(
    [(dy, dx) for dy in range(SIDE) for dx in range(SIDE) if (dy, dx) != (0, 0)],
    key=lambda o: -(ring_distance(o[0]) + ring_distance(o[1])),
)


GROUPS = [(0, 0)] + list(reversed(OFFSETS))
SENT = list(reversed(range(len(OFFSETS))))


def product_kernel(
    shifts, widths, steps, state_hbm, left_hbm, right_hbm,
    upd, w_out,
    state, ext0, ext1, left, right, half, total, sibout, sibin, sums, arrived,
    plane_sem, load_sem, z1_recv, f1_recv, sib_recv, rs_recv, ag_recv, agf_recv, z2_recv, z2f_recv,
    z1_send, early_send, sib_send, rs_send, ag_send, agf_send, z2_send, z2f_send,
):
    ext = (ext0, ext1)
    sectors = lax.axis_size("sec")
    z = lax.axis_index("sec")
    chan = lax.axis_index("chan")
    core = lax.rem(chan, 2)
    chip = chan // 2
    y, x = chip // SIDE, lax.rem(chip, SIDE)
    sib = chan + 1 - 2 * core
    channels = left_hbm.shape[0]
    pad = state_hbm.shape[1]
    wide = pad // 2
    slots = (0, 2)
    targets = (lax.rem(z + 1, sectors), lax.rem(z + sectors - 1, sectors))
    inner = (z < sectors - 1, z > 0)
    end = (z == 0) | (z == sectors - 1)

    def peer(dy, dx):
        return lax.rem(y + dy, SIDE) * SIDE + lax.rem(x + dx, SIDE)

    def remote(src, dst, send, recv, where, there):
        return pltpu.make_async_remote_copy(
            src, dst, send, recv, device_id=(where, there), device_id_type=MESH
        )

    def wait_bytes(ref, sem):
        pltpu.make_async_copy(ref, ref, sem).wait()

    load = pltpu.make_async_copy(state_hbm.at[0], state, load_sem.at[0])
    load.start()
    barrier = pltpu.get_barrier_semaphore()
    for d in range(2):
        @pl.when(inner[d])
        def _():
            pl.semaphore_signal(barrier, 1, device_id=(targets[d], chan), device_id_type=MESH)
    pl.semaphore_signal(barrier, 1, device_id=(z, sib), device_id_type=MESH)
    for step in range(1, SIDE):
        for there in (peer(0, step), peer(step, 0)):
            pl.semaphore_signal(barrier, 1, device_id=(z, there * 2 + core), device_id_type=MESH)

    load.wait()
    width = widths[0]
    rows_at = lax.broadcasted_iota(jnp.int32, (pad, wide), 0)
    cols_at = lax.broadcasted_iota(jnp.int32, (pad, wide), 1)
    for j in range(2):
        kept = (rows_at < width) & (cols_at < width - j * wide)
        values = state[:, pl.ds(j * wide, wide)].astype(F32)
        ext[j][1] = jnp.where(kept, values, 0.0).astype(BF16)

    for slot, at_end in ((0, z == 0), (2, z == sectors - 1)):
        @pl.when(at_end)
        def _():
            ext0[slot] = jnp.zeros((pad, wide), BF16)
            ext1[slot] = jnp.zeros((pad, wide), BF16)
            upd[slot] = jnp.zeros(upd.shape[1:], BF16)

    part = pl.ds(pl.multiple_of(core * wide, wide), wide)
    other = pl.ds(pl.multiple_of((1 - core) * wide, wide), wide)

    def halo(j, d):
        return remote(
            ext[j].at[1, part], ext[j].at[slots[d], part],
            z1_send.at[j, d], z1_recv.at[j, d], targets[d], chan,
        )

    def handed(j, d, rows):
        return remote(
            ext[j].at[slots[d], rows], ext[j].at[slots[d], rows],
            early_send, f1_recv.at[j, d], z, sib,
        )

    @pl.when(end)
    def _():
        pl.semaphore_wait(barrier, 2 * SIDE)

    @pl.when(jnp.logical_not(end))
    def _():
        pl.semaphore_wait(barrier, 2 * SIDE + 1)

    for d in range(2):
        pl.when(inner[d])(halo(0, d).start)
    for step in range(1, SIDE):
        pl.semaphore_signal(plane_sem, 1, device_id=(z, peer(0, step) * 2 + core), device_id_type=MESH)
    loads = [pltpu.make_async_copy(left_hbm.at[:, 0], left, load_sem.at[1])]
    for j in range(2):
        loads.append(
            pltpu.make_async_copy(
                right_hbm.at[:, 0, :, pl.ds(j * wide, wide)], right.at[j], load_sem.at[2 + j]
            )
        )
    for copy in loads:
        copy.start()
    for d in range(2):
        pl.when(inner[d])(halo(0, d).wait_send)
    for d in range(2):
        pl.when(inner[d])(halo(1, d).start)

    for copy in loads:
        copy.wait()

    def hand_over(j):
        for d in range(2):
            @pl.when(inner[1 - d])
            def _():
                halo(j, d).wait_recv()
                handed(j, d, part).start()

    def pair_sent(r):
        here = pl.ds(r * CHIPS // 2, CHIPS // 2)
        return remote(sibout.at[here], sibin.at[here], sib_send, sib_recv.at[r], z, sib)

    hand_over(0)
    for j in range(2):
        for d in range(2):
            pl.when(inner[1 - d])(handed(j, d, other).wait_recv)
        for c in range(channels):
            source = ext[j][1 - shifts[c]]
            half[:, pl.ds(c * wide, wide)] = jnp.dot(
                left[c], source, preferred_element_type=F32
            ).astype(BF16)
        for r in range(2):
            beside = jnp.concatenate([right[j, c] for c in range(channels)], axis=1)
            value = lax.dot_general(
                half[pl.ds(r * wide, wide), :], beside, NT, preferred_element_type=F32
            ).reshape(CHIPS // 2, 2, ROWS, pad)
            here = pl.ds(r * CHIPS // 2, CHIPS // 2)
            if j == 0:
                total[here] = value
                if r == 0:
                    hand_over(1)
            else:
                total[here] = total[here] + value
                sibout[here] = total[here, 1 - core].astype(BF16)
                pair_sent(r).start()

    for r in range(2):
        here = pl.ds(r * CHIPS // 2, CHIPS // 2)
        pair_sent(r).wait_recv()
        pair = total[here, core] + sibin[here].astype(F32)
        sums[here] = pair.astype(BF16)
        total[here, core] = pair
    pl.semaphore_wait(plane_sem, SIDE - 1)
    for i, (dy, dx) in enumerate(OFFSETS):
        there = peer(dy, dx)
        remote(sums.at[there], arrived.at[i], rs_send, rs_recv, z, there * 2 + core).start()

    first = pl.multiple_of(chan * ROWS, ROWS)
    mine = pl.ds(first, ROWS)
    row_ids = first + lax.broadcasted_iota(jnp.int32, (ROWS, pad), 0)
    col_ids = lax.broadcasted_iota(jnp.int32, (ROWS, pad), 1)
    before = jnp.concatenate([ext0[1, mine, :], ext1[1, mine, :]], axis=1).astype(F32)
    acc = total[chip, core]
    wait_bytes(arrived, rs_recv)
    for i in range(len(OFFSETS)):
        acc = acc + arrived[i].astype(F32)
    corrected = jnp.where((row_ids < width) & (col_ids < width), before - steps[0] * acc, 0.0)
    upd[1, chip, core] = corrected.astype(BF16)

    def group(slot, g, parity):
        return upd.at[slot, peer(*GROUPS[g]), parity]

    def gathered(i, where):
        dy, dx = OFFSETS[i]
        block = upd.at[1, where, core]
        return remote(block, block, ag_send, ag_recv.at[i], z, peer(dy, dx) * 2 + core)

    def take(gy, gx):
        i = OFFSETS.index(((SIDE - gy) % SIDE, (SIDE - gx) % SIDE))
        gathered(i, peer(gy, gx)).wait_recv()

    def over_z(g, d):
        return remote(
            group(1, g, core), group(slots[d], g, core),
            z2_send, z2_recv.at[d, GROUPS[g][0]], targets[d], chan,
        )

    def z_on(g):
        for d in range(2):
            pl.when(inner[d])(over_z(g, d).start)

    z_on(0)
    for i in SENT:
        gathered(i, chip).start()
    for g in range(1, len(GROUPS)):
        take(*GROUPS[g])
        z_on(g)
    own_rows = upd.at[1, :, core]
    remote(own_rows, own_rows, agf_send, agf_recv, z, sib).start()
    wait_bytes(upd.at[1, :, 1 - core], agf_recv)

    def chip_row(gy, d, parity):
        rows = pl.ds(pl.multiple_of(lax.rem(y + gy, SIDE) * SIDE, SIDE), SIDE)
        return upd.at[slots[d], rows, parity]

    def hand_row(gy):
        for d in range(2):
            @pl.when(inner[1 - d])
            def _():
                block = chip_row(gy, d, core)
                wait_bytes(block, z2_recv.at[d, gy])
                remote(block, block, z2f_send, z2f_recv, z, sib).start()

    hand_row(0)
    turned = upd[1].reshape(pad, pad).T
    for c in range(channels):
        if c == channels // 2:
            hand_row(1)
            hand_row(3)
        w_out[c] = jnp.dot(turned, left[c], preferred_element_type=F32).astype(BF16)
    hand_row(2)
    for sem, ref in ((sib_send, sibout), (rs_send, arrived), (ag_send, arrived), (agf_send, sums)):
        wait_bytes(ref, sem)

    for d in range(2):
        pl.when(inner[d])(halo(1, d).wait_send)

    @pl.when(end)
    def _():
        wait_bytes(sums, early_send)
        for sem in (z2_send, z2f_send, z2f_recv):
            wait_bytes(sums, sem)

    @pl.when(jnp.logical_not(end))
    def _():
        wait_bytes(left.at[0], early_send)
        for sem in (z2_send, z2f_send, z2f_recv):
            wait_bytes(left.at[0], sem)


def rotate_kernel(scale, shifts, w, upd, rows_out, out, done, sem):
    channels, pad, _ = w.shape
    chan = lax.axis_index("chan")
    rows = pltpu.make_async_copy(
        upd.at[1, chan // 2, lax.rem(chan, 2)], rows_out.at[0], sem.at[channels]
    )
    rows.start()
    copies = [pltpu.make_async_copy(done.at[c], out.at[c, 0], sem.at[c]) for c in range(channels)]
    for c in range(channels):
        source = upd[1 - shifts[c]].reshape(pad, pad)
        done[c] = (jnp.dot(w[c], source, preferred_element_type=F32) * scale).astype(BF16)
        copies[c].start()
    rows.wait()
    for copy in copies:
        copy.wait()


def shards(state_blocks, left_blocks, right_blocks, widths, step_sizes, shifts):
    channels, _, pad, _ = left_blocks.shape
    wide = pad // 2
    n = len(OFFSETS)
    smem = pl.BlockSpec(memory_space=pltpu.SMEM)
    hbm = pl.BlockSpec(memory_space=pltpu.HBM)
    vmem = pl.BlockSpec(memory_space=pltpu.VMEM)
    dma = pltpu.SemaphoreType.DMA
    scalars = pltpu.with_memory_space_constraint(shifts, pltpu.HBM)
    blocks = (pltpu.with_memory_space_constraint(a, pltpu.HBM) for a in (state_blocks, left_blocks, right_blocks))
    upd, turned = pl.pallas_call(
        product_kernel,
        name="product",
        out_shape=(
            jax.ShapeDtypeStruct((3, CHIPS, 2, ROWS, pad), BF16),
            jax.ShapeDtypeStruct((channels, pad, pad), BF16),
        ),
        in_specs=[smem] * 3 + [hbm] * 3,
        out_specs=(vmem, vmem),
        scratch_shapes=[
            pltpu.VMEM((pad, pad), BF16),
            pltpu.VMEM((3, pad, wide), BF16),
            pltpu.VMEM((3, pad, wide), BF16),
            pltpu.VMEM((channels, pad, pad), BF16),
            pltpu.VMEM((2, channels, pad, wide), BF16),
            pltpu.VMEM((pad, channels * wide), BF16),
            pltpu.VMEM((CHIPS, 2, ROWS, pad), F32),
            pltpu.VMEM((CHIPS, ROWS, pad), BF16),
            pltpu.VMEM((CHIPS, ROWS, pad), BF16),
            pltpu.VMEM((CHIPS, ROWS, pad), BF16),
            pltpu.VMEM((n, ROWS, pad), BF16),
            pltpu.SemaphoreType.REGULAR, dma((4,)), dma((2, 2)), dma((2, 2)), dma((2,)), dma(()), dma((n,)), dma(()), dma((2, SIDE)), dma(()),
            dma((2, 2)), *[dma(())] * 7,
        ],
        compiler_params=pltpu.CompilerParams(
            collective_id=0, has_side_effects=True, vmem_limit_bytes=32 << 20
        ),
        cost_estimate=pl.CostEstimate(flops=6 << 30, bytes_accessed=16 << 20, transcendentals=0),
    )(scalars, widths, step_sizes, *blocks)

    rows, new_left = pl.pallas_call(
        functools.partial(rotate_kernel, pad ** (-0.5)),
        name="rotate",
        out_shape=(
            jax.ShapeDtypeStruct((1, ROWS, pad), BF16),
            jax.ShapeDtypeStruct((channels, 1, pad, pad), BF16),
        ),
        in_specs=[smem, vmem, vmem],
        out_specs=(hbm, hbm),
        scratch_shapes=[
            pltpu.VMEM((channels, pad, pad), BF16),
            dma((channels + 1,)),
        ],
        compiler_params=pltpu.CompilerParams(vmem_limit_bytes=16 << 20),
        cost_estimate=pl.CostEstimate(flops=2 << 30, bytes_accessed=10 << 20, transcendentals=0),
    )(scalars, turned, upd)
    return rows, new_left


def solution(mesh):
    placed = (
        P("sec", None, None),
        P("chan", "sec", None, None),
        P("chan", "sec", None, None),
        P("sec"),
        P("sec"),
        P("chan"),
    )
    return jax.shard_map(
        shards,
        mesh=mesh,
        in_specs=placed,
        out_specs=(P("sec", "chan", None), P("chan", "sec", None, None)),
        check_vma=False,
    )
```

```python
import functools

import jax
import jax.numpy as jnp
from jax import lax
from jax.experimental import pallas as pl
from jax.experimental.pallas import tpu as pltpu
from jax.sharding import PartitionSpec as P

MESH = pl.DeviceIdType.MESH
BF16 = jnp.bfloat16
F32 = jnp.float32
NT = (((1,), (1,)), ((), ()))
SIDE = 4
CHIPS = SIDE * SIDE
ROWS = 16


def ring_distance(step):
    return min(step, SIDE - step)


OFFSETS = sorted(
    [(dy, dx) for dy in range(SIDE) for dx in range(SIDE) if (dy, dx) != (0, 0)],
    key=lambda o: -(ring_distance(o[0]) + ring_distance(o[1])),
)


GROUPS = [(0, 0)] + list(reversed(OFFSETS))
SENT = list(reversed(range(len(OFFSETS))))


def product_kernel(
    shifts, widths, steps, state_hbm, left_hbm, right_hbm,
    upd, w_out,
    state, ext0, ext1, left, right, half, total, sibout, sibin, sums, arrived,
    plane_sem, load_sem, z1_recv, f1_recv, sib_recv, rs_recv, ag_recv, agf_recv, z2_recv, z2f_recv,
    z1_send, early_send, sib_send, rs_send, ag_send, agf_send, z2_send, z2f_send,
):
    ext = (ext0, ext1)
    sectors = lax.axis_size("sec")
    z = lax.axis_index("sec")
    chan = lax.axis_index("chan")
    core = lax.rem(chan, 2)
    chip = chan // 2
    y, x = chip // SIDE, lax.rem(chip, SIDE)
    sib = chan + 1 - 2 * core
    channels = left_hbm.shape[0]
    pad = state_hbm.shape[1]
    wide = pad // 2
    slots = (0, 2)
    targets = (lax.rem(z + 1, sectors), lax.rem(z + sectors - 1, sectors))
    inner = (z < sectors - 1, z > 0)
    end = (z == 0) | (z == sectors - 1)

    def peer(dy, dx):
        return lax.rem(y + dy, SIDE) * SIDE + lax.rem(x + dx, SIDE)

    def remote(src, dst, send, recv, where, there):
        return pltpu.make_async_remote_copy(
            src, dst, send, recv, device_id=(where, there), device_id_type=MESH
        )

    def wait_bytes(ref, sem):
        pltpu.make_async_copy(ref, ref, sem).wait()

    load = pltpu.make_async_copy(state_hbm.at[0], state, load_sem.at[0])
    load.start()
    barrier = pltpu.get_barrier_semaphore()
    for d in range(2):
        @pl.when(inner[d])
        def _():
            pl.semaphore_signal(barrier, 1, device_id=(targets[d], chan), device_id_type=MESH)
    pl.semaphore_signal(barrier, 1, device_id=(z, sib), device_id_type=MESH)
    for step in range(1, SIDE):
        for there in (peer(0, step), peer(step, 0)):
            pl.semaphore_signal(barrier, 1, device_id=(z, there * 2 + core), device_id_type=MESH)

    load.wait()
    width = widths[0]
    rows_at = lax.broadcasted_iota(jnp.int32, (pad, wide), 0)
    cols_at = lax.broadcasted_iota(jnp.int32, (pad, wide), 1)
    for j in range(2):
        kept = (rows_at < width) & (cols_at < width - j * wide)
        values = state[:, pl.ds(j * wide, wide)].astype(F32)
        ext[j][1] = jnp.where(kept, values, 0.0).astype(BF16)

    for slot, at_end in ((0, z == 0), (2, z == sectors - 1)):
        @pl.when(at_end)
        def _():
            ext0[slot] = jnp.zeros((pad, wide), BF16)
            ext1[slot] = jnp.zeros((pad, wide), BF16)
            upd[slot] = jnp.zeros(upd.shape[1:], BF16)

    part = pl.ds(pl.multiple_of(core * wide, wide), wide)
    other = pl.ds(pl.multiple_of((1 - core) * wide, wide), wide)

    def halo(j, d):
        return remote(
            ext[j].at[1, part], ext[j].at[slots[d], part],
            z1_send.at[j, d], z1_recv.at[j, d], targets[d], chan,
        )

    def handed(j, d, rows):
        return remote(
            ext[j].at[slots[d], rows], ext[j].at[slots[d], rows],
            early_send, f1_recv.at[j, d], z, sib,
        )

    @pl.when(end)
    def _():
        pl.semaphore_wait(barrier, 2 * SIDE)

    @pl.when(jnp.logical_not(end))
    def _():
        pl.semaphore_wait(barrier, 2 * SIDE + 1)

    for d in range(2):
        pl.when(inner[d])(halo(0, d).start)
    for step in range(1, SIDE):
        pl.semaphore_signal(plane_sem, 1, device_id=(z, peer(0, step) * 2 + core), device_id_type=MESH)
    loads = [pltpu.make_async_copy(left_hbm.at[:, 0], left, load_sem.at[1])]
    for j in range(2):
        loads.append(
            pltpu.make_async_copy(
                right_hbm.at[:, 0, :, pl.ds(j * wide, wide)], right.at[j], load_sem.at[2 + j]
            )
        )
    for copy in loads:
        copy.start()
    for d in range(2):
        pl.when(inner[d])(halo(0, d).wait_send)
    for d in range(2):
        pl.when(inner[d])(halo(1, d).start)

    for copy in loads:
        copy.wait()

    def hand_over(j):
        for d in range(2):
            @pl.when(inner[1 - d])
            def _():
                halo(j, d).wait_recv()
                handed(j, d, part).start()

    def pair_sent(r):
        here = pl.ds(r * CHIPS // 2, CHIPS // 2)
        return remote(sibout.at[here], sibin.at[here], sib_send, sib_recv.at[r], z, sib)

    hand_over(0)
    for j in range(2):
        for d in range(2):
            pl.when(inner[1 - d])(handed(j, d, other).wait_recv)
        for c in range(channels):
            source = ext[j][1 - shifts[c]]
            half[:, pl.ds(c * wide, wide)] = jnp.dot(
                left[c], source, preferred_element_type=F32
            ).astype(BF16)
        for r in range(2):
            beside = jnp.concatenate([right[j, c] for c in range(channels)], axis=1)
            value = lax.dot_general(
                half[pl.ds(r * wide, wide), :], beside, NT, preferred_element_type=F32
            ).reshape(CHIPS // 2, 2, ROWS, pad)
            here = pl.ds(r * CHIPS // 2, CHIPS // 2)
            if j == 0:
                total[here] = value
                if r == 0:
                    hand_over(1)
            else:
                total[here] = total[here] + value
                sibout[here] = total[here, 1 - core].astype(BF16)
                pair_sent(r).start()

    pl.semaphore_wait(plane_sem, SIDE - 1)
    for r in range(2):
        here = pl.ds(r * CHIPS // 2, CHIPS // 2)
        pair_sent(r).wait_recv()
        pair = total[here, core] + sibin[here].astype(F32)
        sums[here] = pair.astype(BF16)
        total[here, core] = pair
        for i, (dy, dx) in enumerate(OFFSETS):
            there = peer(dy, dx)

            @pl.when(there // (CHIPS // 2) == r)
            def _():
                remote(
                    sums.at[there], arrived.at[i], rs_send, rs_recv, z, there * 2 + core
                ).start()

    first = pl.multiple_of(chan * ROWS, ROWS)
    mine = pl.ds(first, ROWS)
    row_ids = first + lax.broadcasted_iota(jnp.int32, (ROWS, pad), 0)
    col_ids = lax.broadcasted_iota(jnp.int32, (ROWS, pad), 1)
    before = jnp.concatenate([ext0[1, mine, :], ext1[1, mine, :]], axis=1).astype(F32)
    acc = total[chip, core]
    wait_bytes(arrived, rs_recv)
    for i in range(len(OFFSETS)):
        acc = acc + arrived[i].astype(F32)
    corrected = jnp.where((row_ids < width) & (col_ids < width), before - steps[0] * acc, 0.0)
    upd[1, chip, core] = corrected.astype(BF16)

    def group(slot, g, parity):
        return upd.at[slot, peer(*GROUPS[g]), parity]

    def gathered(i, where):
        dy, dx = OFFSETS[i]
        block = upd.at[1, where, core]
        return remote(block, block, ag_send, ag_recv.at[i], z, peer(dy, dx) * 2 + core)

    def take(gy, gx):
        i = OFFSETS.index(((SIDE - gy) % SIDE, (SIDE - gx) % SIDE))
        gathered(i, peer(gy, gx)).wait_recv()

    def over_z(g, d):
        return remote(
            group(1, g, core), group(slots[d], g, core),
            z2_send, z2_recv.at[d, GROUPS[g][0]], targets[d], chan,
        )

    def z_on(g):
        for d in range(2):
            pl.when(inner[d])(over_z(g, d).start)

    z_on(0)
    for i in SENT:
        gathered(i, chip).start()
    for g in range(1, len(GROUPS)):
        take(*GROUPS[g])
        z_on(g)
    own_rows = upd.at[1, :, core]
    remote(own_rows, own_rows, agf_send, agf_recv, z, sib).start()
    wait_bytes(upd.at[1, :, 1 - core], agf_recv)

    def chip_row(gy, d, parity):
        rows = pl.ds(pl.multiple_of(lax.rem(y + gy, SIDE) * SIDE, SIDE), SIDE)
        return upd.at[slots[d], rows, parity]

    def hand_row(gy):
        for d in range(2):
            @pl.when(inner[1 - d])
            def _():
                block = chip_row(gy, d, core)
                wait_bytes(block, z2_recv.at[d, gy])
                remote(block, block, z2f_send, z2f_recv, z, sib).start()

    for gy in (0, 1, 3, 2):
        hand_row(gy)
    turned = upd[1].reshape(pad, pad).T
    for c in range(channels):
        w_out[c] = jnp.dot(turned, left[c], preferred_element_type=F32).astype(BF16)
    for sem, ref in ((sib_send, sibout), (rs_send, arrived), (ag_send, arrived), (agf_send, sums)):
        wait_bytes(ref, sem)

    for d in range(2):
        pl.when(inner[d])(halo(1, d).wait_send)

    @pl.when(end)
    def _():
        wait_bytes(sums, early_send)
        for sem in (z2_send, z2f_send, z2f_recv):
            wait_bytes(sums, sem)

    @pl.when(jnp.logical_not(end))
    def _():
        wait_bytes(left.at[0], early_send)
        for sem in (z2_send, z2f_send, z2f_recv):
            wait_bytes(left.at[0], sem)


def rotate_kernel(scale, shifts, w, upd, rows_out, out, done, sem):
    channels, pad, _ = w.shape
    chan = lax.axis_index("chan")
    rows = pltpu.make_async_copy(
        upd.at[1, chan // 2, lax.rem(chan, 2)], rows_out.at[0], sem.at[channels]
    )
    rows.start()
    copies = [pltpu.make_async_copy(done.at[c], out.at[c, 0], sem.at[c]) for c in range(channels)]
    for c in range(channels):
        source = upd[1 - shifts[c]].reshape(pad, pad)
        done[c] = (jnp.dot(w[c], source, preferred_element_type=F32) * scale).astype(BF16)
        copies[c].start()
    rows.wait()
    for copy in copies:
        copy.wait()


def shards(state_blocks, left_blocks, right_blocks, widths, step_sizes, shifts):
    channels, _, pad, _ = left_blocks.shape
    wide = pad // 2
    n = len(OFFSETS)
    smem = pl.BlockSpec(memory_space=pltpu.SMEM)
    hbm = pl.BlockSpec(memory_space=pltpu.HBM)
    vmem = pl.BlockSpec(memory_space=pltpu.VMEM)
    dma = pltpu.SemaphoreType.DMA
    scalars = pltpu.with_memory_space_constraint(shifts, pltpu.HBM)
    blocks = (pltpu.with_memory_space_constraint(a, pltpu.HBM) for a in (state_blocks, left_blocks, right_blocks))
    upd, turned = pl.pallas_call(
        product_kernel,
        name="product",
        out_shape=(
            jax.ShapeDtypeStruct((3, CHIPS, 2, ROWS, pad), BF16),
            jax.ShapeDtypeStruct((channels, pad, pad), BF16),
        ),
        in_specs=[smem] * 3 + [hbm] * 3,
        out_specs=(vmem, vmem),
        scratch_shapes=[
            pltpu.VMEM((pad, pad), BF16),
            pltpu.VMEM((3, pad, wide), BF16),
            pltpu.VMEM((3, pad, wide), BF16),
            pltpu.VMEM((channels, pad, pad), BF16),
            pltpu.VMEM((2, channels, pad, wide), BF16),
            pltpu.VMEM((pad, channels * wide), BF16),
            pltpu.VMEM((CHIPS, 2, ROWS, pad), F32),
            pltpu.VMEM((CHIPS, ROWS, pad), BF16),
            pltpu.VMEM((CHIPS, ROWS, pad), BF16),
            pltpu.VMEM((CHIPS, ROWS, pad), BF16),
            pltpu.VMEM((n, ROWS, pad), BF16),
            pltpu.SemaphoreType.REGULAR, dma((4,)), dma((2, 2)), dma((2, 2)), dma((2,)), dma(()), dma((n,)), dma(()), dma((2, SIDE)), dma(()),
            dma((2, 2)), *[dma(())] * 7,
        ],
        compiler_params=pltpu.CompilerParams(
            collective_id=0, has_side_effects=True, vmem_limit_bytes=32 << 20
        ),
        cost_estimate=pl.CostEstimate(flops=6 << 30, bytes_accessed=16 << 20, transcendentals=0),
    )(scalars, widths, step_sizes, *blocks)

    rows, new_left = pl.pallas_call(
        functools.partial(rotate_kernel, pad ** (-0.5)),
        name="rotate",
        out_shape=(
            jax.ShapeDtypeStruct((1, ROWS, pad), BF16),
            jax.ShapeDtypeStruct((channels, 1, pad, pad), BF16),
        ),
        in_specs=[smem, vmem, vmem],
        out_specs=(hbm, hbm),
        scratch_shapes=[
            pltpu.VMEM((channels, pad, pad), BF16),
            dma((channels + 1,)),
        ],
        compiler_params=pltpu.CompilerParams(vmem_limit_bytes=16 << 20),
        cost_estimate=pl.CostEstimate(flops=2 << 30, bytes_accessed=10 << 20, transcendentals=0),
    )(scalars, turned, upd)
    return rows, new_left


def solution(mesh):
    placed = (
        P("sec", None, None),
        P("chan", "sec", None, None),
        P("chan", "sec", None, None),
        P("sec"),
        P("sec"),
        P("chan"),
    )
    return jax.shard_map(
        shards,
        mesh=mesh,
        in_specs=placed,
        out_specs=(P("sec", "chan", None), P("chan", "sec", None, None)),
        check_vma=False,
    )
```

```python
import functools

import jax
import jax.numpy as jnp
from jax import lax
from jax.experimental import pallas as pl
from jax.experimental.pallas import tpu as pltpu
from jax.sharding import PartitionSpec as P

MESH = pl.DeviceIdType.MESH
BF16 = jnp.bfloat16
F32 = jnp.float32
NT = (((1,), (1,)), ((), ()))
SIDE = 4
CHIPS = SIDE * SIDE
ROWS = 16


def ring_distance(step):
    return min(step, SIDE - step)


OFFSETS = sorted(
    [(dy, dx) for dy in range(SIDE) for dx in range(SIDE) if (dy, dx) != (0, 0)],
    key=lambda o: -(ring_distance(o[0]) + ring_distance(o[1])),
)


GROUPS = [(0, 0)] + list(reversed(OFFSETS))
SENT = list(reversed(range(len(OFFSETS))))


def product_kernel(
    shifts, widths, steps, state_hbm, left_hbm, right_hbm,
    upd, w_out,
    state, ext0, ext1, left, right, half, total, sibout, sibin, sums, arrived,
    plane_sem, load_sem, z1_recv, f1_recv, sib_recv, rs_recv, ag_recv, agf_recv, z2_recv, z2f_recv,
    z1_send, early_send, sib_send, rs_send, ag_send, agf_send, z2_send, z2f_send,
):
    ext = (ext0, ext1)
    sectors = lax.axis_size("sec")
    z = lax.axis_index("sec")
    chan = lax.axis_index("chan")
    core = lax.rem(chan, 2)
    chip = chan // 2
    y, x = chip // SIDE, lax.rem(chip, SIDE)
    sib = chan + 1 - 2 * core
    channels = left_hbm.shape[0]
    pad = state_hbm.shape[1]
    wide = pad // 2
    slots = (0, 2)
    targets = (lax.rem(z + 1, sectors), lax.rem(z + sectors - 1, sectors))
    inner = (z < sectors - 1, z > 0)
    end = (z == 0) | (z == sectors - 1)

    def peer(dy, dx):
        return lax.rem(y + dy, SIDE) * SIDE + lax.rem(x + dx, SIDE)

    def remote(src, dst, send, recv, where, there):
        return pltpu.make_async_remote_copy(
            src, dst, send, recv, device_id=(where, there), device_id_type=MESH
        )

    def wait_bytes(ref, sem):
        pltpu.make_async_copy(ref, ref, sem).wait()

    load = pltpu.make_async_copy(state_hbm.at[0], state, load_sem.at[0])
    load.start()
    barrier = pltpu.get_barrier_semaphore()
    for d in range(2):
        @pl.when(inner[d])
        def _():
            pl.semaphore_signal(barrier, 1, device_id=(targets[d], chan), device_id_type=MESH)
    pl.semaphore_signal(barrier, 1, device_id=(z, sib), device_id_type=MESH)
    for step in range(1, SIDE):
        for there in (peer(0, step), peer(step, 0)):
            pl.semaphore_signal(barrier, 1, device_id=(z, there * 2 + core), device_id_type=MESH)

    loads = [pltpu.make_async_copy(left_hbm.at[:, 0], left, load_sem.at[1])]
    for j in range(2):
        loads.append(
            pltpu.make_async_copy(
                right_hbm.at[:, 0, :, pl.ds(j * wide, wide)], right.at[j], load_sem.at[2 + j]
            )
        )
    for copy in loads:
        copy.start()
    load.wait()
    width = widths[0]
    rows_at = lax.broadcasted_iota(jnp.int32, (pad, wide), 0)
    cols_at = lax.broadcasted_iota(jnp.int32, (pad, wide), 1)
    for j in range(2):
        kept = (rows_at < width) & (cols_at < width - j * wide)
        values = state[:, pl.ds(j * wide, wide)].astype(F32)
        ext[j][1] = jnp.where(kept, values, 0.0).astype(BF16)

    for slot, at_end in ((0, z == 0), (2, z == sectors - 1)):
        @pl.when(at_end)
        def _():
            ext0[slot] = jnp.zeros((pad, wide), BF16)
            ext1[slot] = jnp.zeros((pad, wide), BF16)
            upd[slot] = jnp.zeros(upd.shape[1:], BF16)

    part = pl.ds(pl.multiple_of(core * wide, wide), wide)
    other = pl.ds(pl.multiple_of((1 - core) * wide, wide), wide)

    def halo(j, d):
        return remote(
            ext[j].at[1, part], ext[j].at[slots[d], part],
            z1_send.at[j, d], z1_recv.at[j, d], targets[d], chan,
        )

    def handed(j, d, rows):
        return remote(
            ext[j].at[slots[d], rows], ext[j].at[slots[d], rows],
            early_send, f1_recv.at[j, d], z, sib,
        )

    @pl.when(end)
    def _():
        pl.semaphore_wait(barrier, 2 * SIDE)

    @pl.when(jnp.logical_not(end))
    def _():
        pl.semaphore_wait(barrier, 2 * SIDE + 1)

    for d in range(2):
        pl.when(inner[d])(halo(0, d).start)
    for step in range(1, SIDE):
        pl.semaphore_signal(plane_sem, 1, device_id=(z, peer(0, step) * 2 + core), device_id_type=MESH)
    for d in range(2):
        pl.when(inner[d])(halo(0, d).wait_send)
    for d in range(2):
        pl.when(inner[d])(halo(1, d).start)

    for copy in loads:
        copy.wait()

    def hand_over(j):
        for d in range(2):
            @pl.when(inner[1 - d])
            def _():
                halo(j, d).wait_recv()
                handed(j, d, part).start()

    def pair_sent(r):
        here = pl.ds(r * CHIPS // 2, CHIPS // 2)
        return remote(sibout.at[here], sibin.at[here], sib_send, sib_recv.at[r], z, sib)

    hand_over(0)
    for j in range(2):
        for d in range(2):
            pl.when(inner[1 - d])(handed(j, d, other).wait_recv)
        for c in range(channels):
            source = ext[j][1 - shifts[c]]
            half[:, pl.ds(c * wide, wide)] = jnp.dot(
                left[c], source, preferred_element_type=F32
            ).astype(BF16)
        if j == 0:
            hand_over(1)
        for r in range(2):
            beside = jnp.concatenate([right[j, c] for c in range(channels)], axis=1)
            value = lax.dot_general(
                half[pl.ds(r * wide, wide), :], beside, NT, preferred_element_type=F32
            ).reshape(CHIPS // 2, 2, ROWS, pad)
            here = pl.ds(r * CHIPS // 2, CHIPS // 2)
            if j == 0:
                total[here] = value
            else:
                total[here] = total[here] + value
                sibout[here] = total[here, 1 - core].astype(BF16)
                pair_sent(r).start()

    pl.semaphore_wait(plane_sem, SIDE - 1)
    for r in range(2):
        here = pl.ds(r * CHIPS // 2, CHIPS // 2)
        pair_sent(r).wait_recv()
        pair = total[here, core] + sibin[here].astype(F32)
        sums[here] = pair.astype(BF16)
        total[here, core] = pair
        for i, (dy, dx) in enumerate(OFFSETS):
            there = peer(dy, dx)

            @pl.when(there // (CHIPS // 2) == r)
            def _():
                remote(
                    sums.at[there], arrived.at[i], rs_send, rs_recv, z, there * 2 + core
                ).start()

    first = pl.multiple_of(chan * ROWS, ROWS)
    mine = pl.ds(first, ROWS)
    row_ids = first + lax.broadcasted_iota(jnp.int32, (ROWS, pad), 0)
    col_ids = lax.broadcasted_iota(jnp.int32, (ROWS, pad), 1)
    before = jnp.concatenate([ext0[1, mine, :], ext1[1, mine, :]], axis=1).astype(F32)
    acc = total[chip, core]
    wait_bytes(arrived, rs_recv)
    for i in range(len(OFFSETS)):
        acc = acc + arrived[i].astype(F32)
    corrected = jnp.where((row_ids < width) & (col_ids < width), before - steps[0] * acc, 0.0)
    upd[1, chip, core] = corrected.astype(BF16)

    def group(slot, g, parity):
        return upd.at[slot, peer(*GROUPS[g]), parity]

    def gathered(i, where):
        dy, dx = OFFSETS[i]
        block = upd.at[1, where, core]
        return remote(block, block, ag_send, ag_recv.at[i], z, peer(dy, dx) * 2 + core)

    def take(gy, gx):
        i = OFFSETS.index(((SIDE - gy) % SIDE, (SIDE - gx) % SIDE))
        gathered(i, peer(gy, gx)).wait_recv()

    def over_z(g, d):
        return remote(
            group(1, g, core), group(slots[d], g, core),
            z2_send, z2_recv.at[d, GROUPS[g][0]], targets[d], chan,
        )

    def z_on(g):
        for d in range(2):
            pl.when(inner[d])(over_z(g, d).start)

    z_on(0)
    for i in SENT:
        gathered(i, chip).start()
    for g in range(1, len(GROUPS)):
        take(*GROUPS[g])
        z_on(g)
    own_rows = upd.at[1, :, core]
    remote(own_rows, own_rows, agf_send, agf_recv, z, sib).start()
    wait_bytes(upd.at[1, :, 1 - core], agf_recv)

    def chip_row(gy, d, parity):
        rows = pl.ds(pl.multiple_of(lax.rem(y + gy, SIDE) * SIDE, SIDE), SIDE)
        return upd.at[slots[d], rows, parity]

    def hand_row(gy):
        for d in range(2):
            @pl.when(inner[1 - d])
            def _():
                block = chip_row(gy, d, core)
                wait_bytes(block, z2_recv.at[d, gy])
                remote(block, block, z2f_send, z2f_recv, z, sib).start()

    for gy in (0, 1, 3, 2):
        hand_row(gy)
    turned = upd[1].reshape(pad, pad).T
    for c in range(channels):
        w_out[c] = jnp.dot(turned, left[c], preferred_element_type=F32).astype(BF16)
    for sem, ref in ((sib_send, sibout), (rs_send, arrived), (ag_send, arrived), (agf_send, sums)):
        wait_bytes(ref, sem)

    for d in range(2):
        pl.when(inner[d])(halo(1, d).wait_send)

    @pl.when(end)
    def _():
        wait_bytes(sums, early_send)
        for sem in (z2_send, z2f_send, z2f_recv):
            wait_bytes(sums, sem)

    @pl.when(jnp.logical_not(end))
    def _():
        wait_bytes(left.at[0], early_send)
        for sem in (z2_send, z2f_send, z2f_recv):
            wait_bytes(left.at[0], sem)


def rotate_kernel(scale, shifts, w, upd, rows_out, out, done, sem):
    channels, pad, _ = w.shape
    chan = lax.axis_index("chan")
    rows = pltpu.make_async_copy(
        upd.at[1, chan // 2, lax.rem(chan, 2)], rows_out.at[0], sem.at[channels]
    )
    rows.start()
    copies = [pltpu.make_async_copy(done.at[c], out.at[c, 0], sem.at[c]) for c in range(channels)]
    for c in range(channels):
        source = upd[1 - shifts[c]].reshape(pad, pad)
        done[c] = (jnp.dot(w[c], source, preferred_element_type=F32) * scale).astype(BF16)
        copies[c].start()
    rows.wait()
    for copy in copies:
        copy.wait()


def shards(state_blocks, left_blocks, right_blocks, widths, step_sizes, shifts):
    channels, _, pad, _ = left_blocks.shape
    wide = pad // 2
    n = len(OFFSETS)
    smem = pl.BlockSpec(memory_space=pltpu.SMEM)
    hbm = pl.BlockSpec(memory_space=pltpu.HBM)
    vmem = pl.BlockSpec(memory_space=pltpu.VMEM)
    dma = pltpu.SemaphoreType.DMA
    scalars = pltpu.with_memory_space_constraint(shifts, pltpu.HBM)
    blocks = (pltpu.with_memory_space_constraint(a, pltpu.HBM) for a in (state_blocks, left_blocks, right_blocks))
    upd, turned = pl.pallas_call(
        product_kernel,
        name="product",
        out_shape=(
            jax.ShapeDtypeStruct((3, CHIPS, 2, ROWS, pad), BF16),
            jax.ShapeDtypeStruct((channels, pad, pad), BF16),
        ),
        in_specs=[smem] * 3 + [hbm] * 3,
        out_specs=(vmem, vmem),
        scratch_shapes=[
            pltpu.VMEM((pad, pad), BF16),
            pltpu.VMEM((3, pad, wide), BF16),
            pltpu.VMEM((3, pad, wide), BF16),
            pltpu.VMEM((channels, pad, pad), BF16),
            pltpu.VMEM((2, channels, pad, wide), BF16),
            pltpu.VMEM((pad, channels * wide), BF16),
            pltpu.VMEM((CHIPS, 2, ROWS, pad), F32),
            pltpu.VMEM((CHIPS, ROWS, pad), BF16),
            pltpu.VMEM((CHIPS, ROWS, pad), BF16),
            pltpu.VMEM((CHIPS, ROWS, pad), BF16),
            pltpu.VMEM((n, ROWS, pad), BF16),
            pltpu.SemaphoreType.REGULAR, dma((4,)), dma((2, 2)), dma((2, 2)), dma((2,)), dma(()), dma((n,)), dma(()), dma((2, SIDE)), dma(()),
            dma((2, 2)), *[dma(())] * 7,
        ],
        compiler_params=pltpu.CompilerParams(
            collective_id=0, has_side_effects=True, vmem_limit_bytes=32 << 20
        ),
        cost_estimate=pl.CostEstimate(flops=6 << 30, bytes_accessed=16 << 20, transcendentals=0),
    )(scalars, widths, step_sizes, *blocks)

    rows, new_left = pl.pallas_call(
        functools.partial(rotate_kernel, pad ** (-0.5)),
        name="rotate",
        out_shape=(
            jax.ShapeDtypeStruct((1, ROWS, pad), BF16),
            jax.ShapeDtypeStruct((channels, 1, pad, pad), BF16),
        ),
        in_specs=[smem, vmem, vmem],
        out_specs=(hbm, hbm),
        scratch_shapes=[
            pltpu.VMEM((channels, pad, pad), BF16),
            dma((channels + 1,)),
        ],
        compiler_params=pltpu.CompilerParams(vmem_limit_bytes=16 << 20),
        cost_estimate=pl.CostEstimate(flops=2 << 30, bytes_accessed=10 << 20, transcendentals=0),
    )(scalars, turned, upd)
    return rows, new_left


def solution(mesh):
    placed = (
        P("sec", None, None),
        P("chan", "sec", None, None),
        P("chan", "sec", None, None),
        P("sec"),
        P("sec"),
        P("chan"),
    )
    return jax.shard_map(
        shards,
        mesh=mesh,
        in_specs=placed,
        out_specs=(P("sec", "chan", None), P("chan", "sec", None, None)),
        check_vma=False,
    )
```
